512 devices in a mesh: section: 4 (over x), space: 128 (over y, z, core).
Axes of the slice: x: 4, y: 8, z: 8, core: 2. Of those that a mesh axis runs over, the one named last changes fastest.
Arguments:
- raster: bfloat16 [4, 512, 128, 256], P(None, 'space'), may hold values from -6 to 6
- row_coef: bfloat16 [4, 15, 512, 128], P('section', None, 'space'), may hold values from -1.5 to 1.5
- col_coef: bfloat16 [4, 15, 128, 512], P('section', None, 'space'), may hold values from -1.5 to 1.5
- norm_gain: bfloat16 [4, 256], P('section'), may hold values from 0.099609375 to 1.8984375
- weight_in: bfloat16 [4, 256, 512], P('section'), may hold values from -0.375 to 0.375
- bias_in: bfloat16 [4, 512], P('section'), may hold values from -3 to 3
- weight_out: bfloat16 [4, 512, 256], P('section'), may hold values from -0.25 to 0.25
- readout: bfloat16 [256], replicated, may hold values from -0.375 to 0.375
Outputs:
- density: float32 [4, 512, 128], P('section', 'space')
The draws below stay inside these ranges and needn't reach their ends.
All inputs are finite; a program needn't handle non-finite values.
Results may differ from the reference program's by a relative error of at most 0.015.
Values may be sent and summed in bfloat16 or wider, within the bound.
A program may use at most 64 MiB of HBM per device.

```python
import jax
import jax.numpy as jnp
from jax import lax

CHANNELS = 256
HIDDEN_SIZE = 512
TAPS = 15
W = 128
H = 512
LAYERS = 4
WINDOWS = 4


def steps_of(own_key, extent, shards, low, largest):
    level, own = 1.0, jax.random.fold_in(own_key, 6)
    for position, shards_of in shards:
        steps = jnp.exp(jax.random.uniform(jax.random.fold_in(own, position), (shards_of,), jnp.float32, low / len(shards), largest / len(shards)))
        level = level * jnp.repeat(steps, extent[position] // shards_of).reshape([-1 if axis == position else 1 for axis in range(len(extent))])
    return level


def centred(stream_key, dims, deviation, reach, shards=(), kind=jnp.bfloat16):
    array = deviation * jax.random.normal(stream_key, dims, jnp.float32)
    if shards:
        array = array * steps_of(stream_key, dims, shards, -0.22, 0.18)
    return jnp.clip(array, -reach, reach).astype(kind)


def setup_inputs(seed: int = 0) -> dict:
    key_list = jax.random.split(jax.random.key(seed), 9)
    raster = centred(key_list[0], (WINDOWS, H, W, CHANNELS), 1.0, 6.0, ((1, 128),))
    row_coef = centred(key_list[1], (LAYERS, TAPS, H, W), TAPS ** -0.5, 1.5, ((0, 4), (2, 128)))
    col_coef = centred(key_list[2], (LAYERS, TAPS, W, H), TAPS ** -0.5, 1.5, ((0, 4), (2, 128)))
    norm_gain = jnp.clip(1.0 + 0.18 * jax.random.normal(key_list[3], (LAYERS, CHANNELS), jnp.float32), 0.099609375, 1.8984375).astype(jnp.bfloat16)
    weight_in = centred(key_list[4], (LAYERS, CHANNELS, HIDDEN_SIZE), CHANNELS ** -0.5, 0.375, ((0, 4),))
    bias_in = centred(key_list[5], (LAYERS, HIDDEN_SIZE), 0.5, 3.0, ((0, 4),))
    weight_out = centred(key_list[6], (LAYERS, HIDDEN_SIZE, CHANNELS), HIDDEN_SIZE ** -0.5, 0.25, ((0, 4),))
    readout = centred(key_list[7], (CHANNELS,), CHANNELS ** -0.5, 0.375)
    return {"raster": raster, "row_coef": row_coef, "col_coef": col_coef, "norm_gain": norm_gain, "weight_in": weight_in, "bias_in": bias_in, "weight_out": weight_out, "readout": readout}


def row_stencil(surface, coefficients):
    taps_count = coefficients.shape[0]
    radius = taps_count // 2
    columns = surface.shape[1]
    padded = jnp.pad(surface.astype(jnp.float32), ((0, 0), (radius, radius), (0, 0)))
    summed = jnp.zeros(surface.shape, jnp.float32)
    for offset in range(taps_count):
        summed = summed + coefficients[offset].astype(jnp.float32)[:, :, None] * padded[:, offset:offset + columns, :]
    return summed

def col_stencil(surface, coefficients):
    taps_count = coefficients.shape[0]
    radius = taps_count // 2
    lines = surface.shape[0]
    swapped = jnp.swapaxes(coefficients, 1, 2)
    padded = jnp.pad(surface.astype(jnp.float32), ((radius, radius), (0, 0), (0, 0)))
    summed = jnp.zeros(surface.shape, jnp.float32)
    for offset in range(taps_count):
        summed = summed + swapped[offset].astype(jnp.float32)[:, :, None] * padded[offset:offset + lines, :, :]
    return summed

def dense_part(mixed_field, norm_gain, weight_in, bias_in, weight_out):
    inverse = lax.rsqrt(lax.optimization_barrier(jnp.mean(mixed_field * mixed_field, axis=-1, keepdims=True)) + 1e-06)
    normed = (mixed_field * inverse * norm_gain.astype(jnp.float32)).astype(jnp.bfloat16)
    hidden = jax.nn.gelu(jnp.dot(normed, weight_in, preferred_element_type=jnp.float32) + bias_in.astype(jnp.float32), approximate=True).astype(jnp.bfloat16)
    return (mixed_field + jnp.dot(hidden, weight_out, preferred_element_type=jnp.float32)).astype(jnp.bfloat16)

def reference(raster, row_coef, col_coef, norm_gain, weight_in, bias_in, weight_out, readout):

    def one_window(surface):
        for layer_index in range(LAYERS):
            row_part = row_stencil(surface, row_coef[layer_index]).astype(jnp.bfloat16)
            mixed_field = col_stencil(row_part, col_coef[layer_index])
            surface = dense_part(mixed_field, norm_gain[layer_index], weight_in[layer_index], bias_in[layer_index], weight_out[layer_index])
        logits = jnp.dot(surface, readout, preferred_element_type=jnp.float32)
        return jax.nn.softplus(logits)
    return lax.map(one_window, raster)
```

```python
import jax
import jax.numpy as jnp
from jax import lax
from jax.experimental import pallas as pl
from jax.experimental.pallas import tpu as pltpu
from jax.sharding import PartitionSpec as P

MESH = pl.DeviceIdType.MESH
F32, BF16 = jnp.float32, jnp.bfloat16
LAYERS, TAPS, RAD = 4, 15, 7
NY, NZ = 8, 8
ROWS = 8
HALF = 64
GROUP = 16
GROUPS = HALF // GROUP
CH, HID = 256, 512
BAND = 24 * GROUP


def remote(src, dst, send_sem, recv_sem, device):
    return pltpu.make_async_remote_copy(
        src_ref=src,
        dst_ref=dst,
        send_sem=send_sem,
        recv_sem=recv_sem,
        device_id=device,
        device_id_type=MESH,
    )


def kernel(
    raster, row_coef, col_coef, gain, w_in, bias, w_out, readout,
    out,
    S, R, A, LHS, WI, WO, RC, TT, CS, CT, ZS, ZB, YS, MC, MN, PB, DS, DR,
    lsem, zs, zr, ys, yr, xs, xr, rcs, rcr, ras, rar, pbs, pbr,
    ws, wr, fs, vs, vr, hs, hr, ss, sr, ds, dr,
):
    s = lax.axis_index("section")
    p = lax.axis_index("space")
    t, c = p // 2, p % 2
    y, z = t // NZ, t % NZ
    partner = (s, t * 2 + 1 - c)

    def sec(ds_):
        return lax.rem(s + ds_, LAYERS)

    def dev(yy, zz, cc):
        return (s, (yy * NZ + zz) * 2 + cc)

    prev_chip = (s, lax.rem(t + NY * NZ - 1, NY * NZ) * 2 + c)
    next_chip = (s, lax.rem(t + 1, NY * NZ) * 2 + c)

    barrier = pltpu.get_barrier_semaphore()
    greeted = []
    for k in range(1, LAYERS):
        greeted += [(sec(k), t * 2 + c), (sec(k), t * 2 + 1 - c)]
    for k in range(1, NZ):
        greeted.append(dev(y, lax.rem(z + k, NZ), c))
    for k in range(1, NY):
        for cc in range(2):
            greeted.append(dev(lax.rem(y + k, NY), z, cc))
    greeted += [partner, prev_chip, next_chip]
    for device in greeted:
        pl.semaphore_signal(barrier, inc=1, device_id=device, device_id_type=MESH)

    mine = pl.multiple_of(48 * c, 16)
    theirs = pl.multiple_of(48 * (1 - c), 16)
    mine_to = pl.multiple_of(16 - 16 * c, 16)
    theirs_to = pl.multiple_of(16 * c, 16)
    own_rows = pl.ds(c * 4, 4)
    loads = [
        pltpu.make_async_copy(
            raster.at[s, :, pl.ds(mine, 80), :],
            S.at[0, own_rows, pl.ds(mine_to, 80), :],
            lsem.at[0],
        ),
        pltpu.make_async_copy(w_in.at[0], WI.at[s], lsem.at[1]),
        pltpu.make_async_copy(w_out.at[0], WO.at[s], lsem.at[2]),
    ]
    for load in loads:
        load.start()

    edge = pl.multiple_of(80 * c, 16)
    for layer in range(LAYERS):
        S[layer, :, pl.ds(edge, 16), :] = jnp.zeros((ROWS, 16, CH), BF16)
        S[layer, :, 96:128, :] = jnp.zeros((ROWS, 32, CH), BF16)
        R[layer, :, 22:24] = jnp.zeros((GROUPS, 2, GROUP, CH), BF16)

        @pl.when(t == 0)
        def _():
            R[layer, :, 0:RAD] = jnp.zeros((GROUPS, RAD, GROUP, CH), BF16)

        @pl.when(t == NY * NZ - 1)
        def _():
            R[layer, :, 15:22] = jnp.zeros((GROUPS, RAD, GROUP, CH), BF16)

    rc = row_coef[0].astype(F32)
    for i in range(4):
        RC[s, c * 4 + i] = jnp.concatenate([rc[:, i, :], jnp.zeros((1, 128), F32)], axis=0)
    PB[s] = jnp.zeros((8, HID), F32)
    PB[s, 0:1, :] = bias[...].astype(F32)
    PB[s, 1:2, 0:CH] = gain[...].astype(F32)
    CS[...] = jnp.zeros(CS.shape, F32)
    CS[0:TAPS, :] = col_coef[0, :, 0, :].astype(F32)
    for q in range(4):
        CT[128 * q : 128 * (q + 1), :] = CS[:, 128 * q : 128 * (q + 1)].T
    for zz in range(NZ):
        total = CT[pl.ds(8 * zz, 8, stride=64), :]
        for r in range(1, ROWS):
            total = total + pltpu.roll(CT[pl.ds(8 * zz + r, 8, stride=64), :], 16 * r, 1)
        ZS[zz] = total

    pl.semaphore_wait(barrier, len(greeted))

    started = []

    def go(copy):
        copy.start()
        started.append(copy)

    for k in range(1, NZ):
        zz = lax.rem(z + k, NZ)
        go(remote(ZS.at[zz], ZB.at[z], zs.at[k], zr.at[k], dev(y, zz, c)))
    half = pl.ds(c * 4, 4)
    rows_sent = [(s, t * 2 + 1 - c)]
    for k in range(1, LAYERS):
        rows_sent += [(sec(k), t * 2 + c), (sec(k), t * 2 + 1 - c)]
    for k, device in enumerate(rows_sent):
        go(remote(RC.at[s, half], RC.at[s, half], rcs.at[k], rcr.at[s, c], device))
    go(
        remote(
            raster.at[s, :, pl.ds(theirs, 80), :],
            S.at[0, own_rows, pl.ds(theirs_to, 80), :],
            ras,
            rar,
            partner,
        )
    )
    for k in range(1, LAYERS):
        go(remote(PB.at[s], PB.at[s], pbs.at[k], pbr.at[s], (sec(k), p)))
    wi_half, wo_half = pl.ds(c * 128, 128), pl.ds(c * 256, 256)
    wi_other, wo_other = pl.ds((1 - c) * 128, 128), pl.ds((1 - c) * 256, 256)
    up, down = (sec(1), p), (sec(3), p)
    for k, device in enumerate((up, down)):
        go(remote(w_in.at[0, wi_half], WI.at[s, wi_half], ws.at[k, 0], wr.at[s, 0], device))
        go(remote(w_out.at[0, wo_half], WO.at[s, wo_half], ws.at[k, 1], wr.at[s, 1], device))

    def got_rows(layer):
        for h in range(2):

            @pl.when(jnp.logical_or(s != layer, c != h))
            def _():
                ref = RC.at[layer, pl.ds(4 * h, 4)]
                remote(ref, ref, rcs.at[0], rcr.at[layer, h], partner).wait_recv()

    lane = lax.broadcasted_iota(jnp.int32, (HALF, 128), 1)

    def build_rows(layer):
        TT[...] = RC[layer].reshape(128, 128).T
        taps = TT[pl.ds(pl.multiple_of(HALF * c, HALF), HALF), :]
        for i in range(ROWS):
            kept = jnp.where(lane // 16 == i, taps, 0.0)
            A[layer, i] = pltpu.roll(kept, (9 - 16 * i) % 128, 1, stride=1, stride_axis=0).astype(
                BF16
            )

    def row_stencil(layer):
        for i in range(ROWS):
            got = jnp.dot(A[layer, i], S[layer, i], preferred_element_type=F32).astype(BF16)
            for g in range(GROUPS):
                R[layer, g, RAD + i] = got[GROUP * g : GROUP * (g + 1)]

    def halo(layer, g, way):
        src, dst, device = ((7, 15, prev_chip), (8, 0, next_chip))[way]
        return remote(
            R.at[layer, g, pl.ds(src, RAD)],
            R.at[layer, g, pl.ds(dst, RAD)],
            hs.at[layer, way, g],
            hr.at[layer, way, g],
            device,
        )

    not_first, not_last = t > 0, t < NY * NZ - 1

    def order(step):
        return jnp.where(c == 0, GROUPS - 1 - step, step)

    def send_halos(layer):
        for step in range(GROUPS):
            g = order(step)

            @pl.when(not_first)
            def _():
                halo(layer, g, 0).start()

            @pl.when(not_last)
            def _():
                halo(layer, g, 1).start()

    def got_halos(layer, g):
        @pl.when(not_last)
        def _():
            halo(layer, g, 0).wait_recv()

        @pl.when(not_first)
        def _():
            halo(layer, g, 1).wait_recv()

    got_rows(0)
    build_rows(0)
    loads[0].wait()
    their_rows = pl.ds((1 - c) * 4, 4)
    remote(
        raster.at[s, :, pl.ds(theirs, 80), :],
        S.at[0, their_rows, pl.ds(mine_to, 80), :],
        ras,
        rar,
        partner,
    ).wait_recv()
    row_stencil(0)
    send_halos(0)

    ZB[z] = ZS[z]
    for k in range(1, NZ):
        remote(
            ZS.at[0], ZB.at[lax.rem(z + NZ - k, NZ)], zs.at[0], zr.at[k], partner
        ).wait_recv()
    d, gy = y // 4, y % 4
    for k in range(NY):
        yy = lax.rem(y + k, NY)
        YS[k] = ZB[pl.ds(0, NZ), yy, :]
        copy = remote(YS.at[k], MC.at[s, gy, c], ys.at[k], yr.at[gy, c], dev(yy, z, d))
        if k > 0:
            go(copy)
        else:

            @pl.when(d != c)
            def _():
                copy.start()

            @pl.when(d == c)
            def _():
                MC[s, gy, c] = YS[0]

            own_y = copy
    for l in range(1, LAYERS):
        got_rows(l)
        build_rows(l)
    for g in range(GROUPS):
        for cc in range(2):
            away = jnp.logical_or(jnp.logical_or(d != c, gy != g), c != cc)

            @pl.when(away)
            def _():
                remote(
                    YS.at[0], MC.at[s, g, cc], ys.at[0], yr.at[g, cc], partner
                ).wait_recv()

    for k in range(1, LAYERS):
        go(remote(MC.at[s], MC.at[s], xs.at[k], xr.at[s], (sec(k), p)))

    def weight_from(layer, piece):
        ref = (WI.at[layer, wi_half], WO.at[layer, wo_half])[piece]
        return remote(ref, ref, ws.at[0, 0], wr.at[layer, piece], partner)

    def pass_on(layer, piece, k):
        ref = (WI.at[layer, wi_half], WO.at[layer, wo_half])[piece]
        go(remote(ref, ref, vs.at[k, piece], vr.at[layer, piece], partner))

    below, above, across = sec(3), sec(1), sec(2)
    for piece in range(2):
        weight_from(below, piece).wait_recv()
        if piece == 0:
            ref = WI.at[below, wi_half]
            go(remote(ref, ref, fs.at[0], wr.at[below, 0], up))
        pass_on(below, piece, 0)
        weight_from(above, piece).wait_recv()
        if piece == 1:
            ref = WO.at[above, wo_half]
            go(remote(ref, ref, fs.at[1], wr.at[above, 1], down))
        pass_on(above, piece, 1)
    for piece in range(2):
        weight_from(across, piece).wait_recv()
        pass_on(across, piece, 2)
    for load in loads[1:]:
        load.wait()

    row_id = lax.broadcasted_iota(jnp.int32, (128, 256), 0)
    lane_id = lax.broadcasted_iota(jnp.int32, (128, 256), 1)
    spread = jnp.where(row_id == lane_id // 16, 1.0, 0.0).astype(BF16)
    spread = jnp.where(row_id < 16, spread, jnp.zeros_like(spread))
    diag = (
        lax.broadcasted_iota(jnp.int32, (HALF, 256), 1) % 16
        == lax.broadcasted_iota(jnp.int32, (HALF, 256), 0) % 16
    )

    def got_cols(layer):
        @pl.when(s != layer)
        def _():
            remote(MC.at[layer], MC.at[layer], xs.at[0], xr.at[layer], partner).wait_recv()
            remote(PB.at[layer], PB.at[layer], pbs.at[0], pbr.at[layer], partner).wait_recv()
            for piece in range(2):
                ref = (WI.at[layer, wi_other], WO.at[layer, wo_other])[piece]
                remote(ref, ref, vs.at[0, 0], vr.at[layer, piece], partner).wait_recv()

    def build_cols(layer):
        for g in range(GROUPS):
            for cc in range(2):
                MN[pl.ds(GROUP * g + cc, 8, stride=2), :] = MC[layer, g, cc]
        taps = MN[...]
        for i in range(ROWS):
            turned = taps if i == 0 else pltpu.roll(taps, 128 - 16 * i, 1)
            wide = jnp.dot(turned.astype(BF16), spread, preferred_element_type=F32)
            wide = jnp.where(diag, wide, 0.0)
            wide = jnp.concatenate([wide, jnp.zeros((HALF, 128), F32)], axis=1)
            if i:
                wide = pltpu.roll(wide, 16 * i, 1)
            wide = wide.astype(BF16)
            for g in range(GROUPS):
                LHS[layer, g, GROUP * i : GROUP * (i + 1), :] = wide[GROUP * g : GROUP * (g + 1)]

    def dense(layer, g):
        field = jnp.dot(
            LHS[layer, g], R[layer, g].reshape(BAND, CH), preferred_element_type=F32
        )
        inverse = lax.rsqrt(jnp.mean(field * field, axis=-1, keepdims=True) + 1e-06)
        normed = (field * inverse * PB[layer, 1:2, 0:CH]).astype(BF16)
        hidden = jax.nn.gelu(
            jnp.dot(normed, WI[layer], preferred_element_type=F32) + PB[layer, 0:1, :],
            approximate=True,
        ).astype(BF16)
        state = (field + jnp.dot(hidden, WO[layer], preferred_element_type=F32)).astype(BF16)
        at = pl.ds(pl.multiple_of(16 + GROUP * g, 16), GROUP)
        for i in range(ROWS):
            S[layer + 1, i, at, :] = state[GROUP * i : GROUP * (i + 1)]

    edge_from = pl.multiple_of(64 - 48 * c, 16)
    edge_to = pl.multiple_of(80 * c, 16)
    edge_in = pl.multiple_of(80 - 80 * c, 16)

    def edge_copy(layer):
        return remote(
            S.at[layer, :, pl.ds(edge_from, 16), :],
            S.at[layer, :, pl.ds(edge_to, 16), :],
            ss.at[layer],
            sr.at[layer],
            partner,
        )

    for layer in range(LAYERS):
        if layer > 0:
            ref = S.at[layer, :, pl.ds(edge_in, 16), :]
            remote(ref, ref, ss.at[layer], sr.at[layer], partner).wait_recv()
            row_stencil(layer)
            send_halos(layer)
        got_cols(layer)
        build_cols(layer)
        for step in range(GROUPS):
            g = order(step)
            got_halos(layer, g)
            dense(layer, g)
            if step == 0 and layer < LAYERS - 1:
                go(edge_copy(layer + 1))

    weights = jnp.broadcast_to(readout[...].astype(F32), (8, CH))
    which = lax.broadcasted_iota(jnp.int32, (8, CH), 0)
    logits = jnp.zeros((8, HALF), F32)
    for i in range(ROWS):
        logits = logits + lax.dot_general(
            jnp.where(which == i, weights, 0.0).astype(BF16),
            S[LAYERS, i, 16 : 16 + HALF, :],
            (((1,), (1,)), ((), ())),
            preferred_element_type=F32,
        )
    values = jax.nn.softplus(jnp.concatenate([logits, logits], axis=1))
    DS[0] = values
    DS[1] = pltpu.roll(values, 4, 0)
    go(remote(DS.at[1 - c], DR, ds, dr, partner))
    remote(DS.at[c], DR, ds, dr, partner).wait_recv()
    cols = lax.broadcasted_iota(jnp.int32, (8, 128), 1)
    out[0] = jnp.where(cols // HALF == c, DS[c], DR[...])[0:4]

    for copy in started:
        copy.wait_send()

    @pl.when(d != c)
    def _():
        own_y.wait_send()

    for layer in range(LAYERS):
        for g in range(GROUPS):

            @pl.when(not_first)
            def _():
                halo(layer, g, 0).wait_send()

            @pl.when(not_last)
            def _():
                halo(layer, g, 1).wait_send()


def on_device(raster, row_coef, col_coef, norm_gain, weight_in, bias_in, weight_out, readout):
    vmem = pl.BlockSpec(memory_space=pltpu.VMEM)
    anywhere = pl.BlockSpec(memory_space=pl.ANY)
    dma = pltpu.SemaphoreType.DMA
    return pl.pallas_call(
        kernel,
        out_shape=jax.ShapeDtypeStruct((1, 4, 128), F32),
        in_specs=[anywhere, vmem, vmem, vmem, anywhere, vmem, anywhere, vmem],
        out_specs=vmem,
        scratch_shapes=[
            pltpu.VMEM((LAYERS + 1, ROWS, 128, CH), BF16),
            pltpu.VMEM((LAYERS, GROUPS, 24, GROUP, CH), BF16),
            pltpu.VMEM((LAYERS, ROWS, HALF, 128), BF16),
            pltpu.VMEM((LAYERS, GROUPS, 128, BAND), BF16),
            pltpu.VMEM((LAYERS, CH, HID), BF16),
            pltpu.VMEM((LAYERS, HID, CH), BF16),
            pltpu.VMEM((LAYERS, ROWS, 16, 128), F32),
            pltpu.VMEM((128, 128), F32),
            pltpu.VMEM((128, 512), F32),
            pltpu.VMEM((512, 128), F32),
            pltpu.VMEM((NZ, 8, 128), F32),
            pltpu.VMEM((NZ, 8, 128), F32),
            pltpu.VMEM((NY, 8, 128), F32),
            pltpu.VMEM((LAYERS, GROUPS, 2, 8, 128), F32),
            pltpu.VMEM((HALF, 128), F32),
            pltpu.VMEM((LAYERS, 8, HID), F32),
            pltpu.VMEM((2, 8, 128), F32),
            pltpu.VMEM((8, 128), F32),
            dma((3,)),
            dma((NZ,)), dma((NZ,)),
            dma((NY,)), dma((GROUPS, 2)),
            dma((LAYERS,)), dma((LAYERS,)),
            dma((7,)), dma((LAYERS, 2)),
            dma, dma,
            dma((LAYERS,)), dma((LAYERS,)),
            dma((2, 2)), dma((LAYERS, 2)), dma((2,)),
            dma((3, 2)), dma((LAYERS, 2)),
            dma((LAYERS, 2, GROUPS)), dma((LAYERS, 2, GROUPS)),
            dma((LAYERS,)), dma((LAYERS,)),
            dma, dma,
        ],
        compiler_params=pltpu.CompilerParams(
            collective_id=0, has_side_effects=True, vmem_limit_bytes=48 * 1024 * 1024
        ),
        name="forecast",
    )(
        raster, row_coef, col_coef, norm_gain, weight_in, bias_in, weight_out,
        readout.reshape(1, CH),
    )


def solution(mesh):
    placed = (
        P(None, "space", None, None),
        P("section", None, "space", None),
        P("section", None, "space", None),
        P("section", None),
        P("section", None, None),
        P("section", None),
        P("section", None, None),
        P(),
    )
    return jax.shard_map(
        on_device,
        mesh=mesh,
        in_specs=placed,
        out_specs=P("section", "space", None),
        check_vma=False,
    )
```

```python
import jax
import jax.numpy as jnp
from jax import lax
from jax.experimental import pallas as pl
from jax.experimental.pallas import tpu as pltpu
from jax.sharding import PartitionSpec as P

MESH = pl.DeviceIdType.MESH
F32, BF16 = jnp.float32, jnp.bfloat16
LAYERS, TAPS, RAD = 4, 15, 7
NY, NZ = 8, 8
ROWS = 8
HALF = 64
GROUP = 16
GROUPS = HALF // GROUP
CH, HID = 256, 512
BAND = 24 * GROUP


def remote(src, dst, send_sem, recv_sem, device):
    return pltpu.make_async_remote_copy(
        src_ref=src,
        dst_ref=dst,
        send_sem=send_sem,
        recv_sem=recv_sem,
        device_id=device,
        device_id_type=MESH,
    )


def kernel(
    raster, row_coef, col_coef, gain, w_in, bias, w_out, readout,
    out,
    S, R, A, LHS, WI, WO, RC, TT, CS, CT, ZS, ZB, YS, MC, MN, PB, DS, DR,
    lsem, zs, zr, ys, yr, rcs, rcr, ras, rar, pbs, pbr,
    ws, wr, fs, vs, vr, hs, hr, ss, sr, ds, dr,
):
    s = lax.axis_index("section")
    p = lax.axis_index("space")
    t, c = p // 2, p % 2
    y, z = t // NZ, t % NZ
    partner = (s, t * 2 + 1 - c)

    def sec(ds_):
        return lax.rem(s + ds_, LAYERS)

    def dev(yy, zz, cc):
        return (s, (yy * NZ + zz) * 2 + cc)

    prev_chip = (s, lax.rem(t + NY * NZ - 1, NY * NZ) * 2 + c)
    next_chip = (s, lax.rem(t + 1, NY * NZ) * 2 + c)

    barrier = pltpu.get_barrier_semaphore()
    greeted = []
    for k in range(LAYERS):
        for j in range(NY):
            yy = lax.rem(y + j, NY)
            for cc in range(2):
                if k or j:
                    greeted.append((sec(k), (yy * NZ + z) * 2 + (c + cc) % 2))
    for k in range(1, NZ):
        greeted.append(dev(y, lax.rem(z + k, NZ), c))
    greeted += [partner, prev_chip, next_chip]
    for device in greeted:
        pl.semaphore_signal(barrier, inc=1, device_id=device, device_id_type=MESH)

    mine = pl.multiple_of(48 * c, 16)
    theirs = pl.multiple_of(48 * (1 - c), 16)
    mine_to = pl.multiple_of(16 - 16 * c, 16)
    theirs_to = pl.multiple_of(16 * c, 16)
    own_rows = pl.ds(c * 4, 4)
    loads = [
        pltpu.make_async_copy(
            raster.at[s, :, pl.ds(mine, 80), :],
            S.at[0, own_rows, pl.ds(mine_to, 80), :],
            lsem.at[0],
        ),
        pltpu.make_async_copy(w_in.at[0], WI.at[s], lsem.at[1]),
        pltpu.make_async_copy(w_out.at[0], WO.at[s], lsem.at[2]),
    ]
    for load in loads:
        load.start()

    edge = pl.multiple_of(80 * c, 16)
    for layer in range(LAYERS):
        S[layer, :, pl.ds(edge, 16), :] = jnp.zeros((ROWS, 16, CH), BF16)
        R[layer, :, 22:24] = jnp.zeros((GROUPS, 2, GROUP, CH), BF16)

        @pl.when(t == 0)
        def _():
            R[layer, :, 0:RAD] = jnp.zeros((GROUPS, RAD, GROUP, CH), BF16)

        @pl.when(t == NY * NZ - 1)
        def _():
            R[layer, :, 15:22] = jnp.zeros((GROUPS, RAD, GROUP, CH), BF16)

    rc = row_coef[0].astype(F32)
    for i in range(4):
        RC[s, c * 4 + i] = jnp.concatenate([rc[:, i, :], jnp.zeros((1, 128), F32)], axis=0)
    PB[s] = jnp.zeros((8, HID), F32)
    PB[s, 0:1, :] = bias[...].astype(F32)
    PB[s, 1:2, 0:CH] = gain[...].astype(F32)
    CS[...] = jnp.zeros(CS.shape, F32)
    CS[0:TAPS, :] = col_coef[0, 0].astype(F32)
    for q in range(4):
        CT[128 * q : 128 * (q + 1), :] = CS[:, 128 * q : 128 * (q + 1)].T
    for zz in range(NZ):
        total = CT[pl.ds(8 * zz, 8, stride=64), :]
        for r in range(1, ROWS):
            total = total + pltpu.roll(CT[pl.ds(8 * zz + r, 8, stride=64), :], 16 * r, 1)
        ZS[zz] = total

    pl.semaphore_wait(barrier, len(greeted))

    started = []

    def go(copy):
        copy.start()
        started.append(copy)

    for k in range(1, NZ):
        zz = lax.rem(z + k, NZ)
        go(remote(ZS.at[zz], ZB.at[z], zs.at[k], zr.at[k], dev(y, zz, c)))
    half = pl.ds(c * 4, 4)
    rows_sent = [(s, t * 2 + 1 - c)]
    for k in range(1, LAYERS):
        rows_sent += [(sec(k), t * 2 + c), (sec(k), t * 2 + 1 - c)]
    for k, device in enumerate(rows_sent):
        go(remote(RC.at[s, half], RC.at[s, half], rcs.at[k], rcr.at[s, c], device))
    go(
        remote(
            raster.at[s, :, pl.ds(theirs, 80), :],
            S.at[0, own_rows, pl.ds(theirs_to, 80), :],
            ras,
            rar,
            partner,
        )
    )
    for k in range(1, LAYERS):
        go(remote(PB.at[s], PB.at[s], pbs.at[k], pbr.at[s], (sec(k), p)))
    wi_half, wo_half = pl.ds(c * 128, 128), pl.ds(c * 256, 256)
    wi_other, wo_other = pl.ds((1 - c) * 128, 128), pl.ds((1 - c) * 256, 256)
    up, down = (sec(1), p), (sec(3), p)
    for k, device in enumerate((up, down)):
        for piece in (k, 1 - k):
            src = (w_in.at[0, wi_half], w_out.at[0, wo_half])[piece]
            dst = (WI.at[s, wi_half], WO.at[s, wo_half])[piece]
            go(remote(src, dst, ws.at[k, piece], wr.at[s, piece], device))

    def got_rows(layer):
        for h in range(2):

            @pl.when(jnp.logical_or(s != layer, c != h))
            def _():
                ref = RC.at[layer, pl.ds(4 * h, 4)]
                remote(ref, ref, rcs.at[0], rcr.at[layer, h], partner).wait_recv()

    lane = lax.broadcasted_iota(jnp.int32, (HALF, 128), 1)

    def build_rows(layer):
        TT[...] = RC[layer].reshape(128, 128).T
        taps = TT[pl.ds(pl.multiple_of(HALF * c, HALF), HALF), :]
        for i in range(ROWS):
            kept = jnp.where(lane // 16 == i, taps, 0.0)
            for g in range(GROUPS):
                A[layer, g, i] = pltpu.roll(
                    kept[GROUP * g : GROUP * (g + 1)],
                    (9 - 16 * i) % 128,
                    1,
                    stride=1,
                    stride_axis=0,
                ).astype(BF16)

    def row_stencil(layer, g):
        window = pl.ds(pl.multiple_of(GROUP * g, GROUP), 3 * GROUP)
        for i in range(ROWS):
            R[layer, g, RAD + i] = jnp.dot(
                A[layer, g, i][:, 0 : 3 * GROUP],
                S[layer, i, window, :],
                preferred_element_type=F32,
            ).astype(BF16)

    def halo(layer, g, way):
        src, dst, device = ((7, 15, prev_chip), (8, 0, next_chip))[way]
        return remote(
            R.at[layer, g, pl.ds(src, RAD)],
            R.at[layer, g, pl.ds(dst, RAD)],
            hs.at[layer, way, g],
            hr.at[layer, way, g],
            device,
        )

    not_first, not_last = t > 0, t < NY * NZ - 1

    def order(step):
        return jnp.where(c == 0, step, GROUPS - 1 - step)

    def send_row(layer, g):
        row_stencil(layer, g)

        @pl.when(not_first)
        def _():
            halo(layer, g, 0).start()

        @pl.when(not_last)
        def _():
            halo(layer, g, 1).start()

    def got_halos(layer, g):
        @pl.when(not_last)
        def _():
            halo(layer, g, 0).wait_recv()

        @pl.when(not_first)
        def _():
            halo(layer, g, 1).wait_recv()

    got_rows(0)
    build_rows(0)
    loads[0].wait()
    their_rows = pl.ds((1 - c) * 4, 4)
    remote(
        raster.at[s, :, pl.ds(theirs, 80), :],
        S.at[0, their_rows, pl.ds(mine_to, 80), :],
        ras,
        rar,
        partner,
    ).wait_recv()
    for step in range(GROUPS):
        send_row(0, order(step))

    ZB[z] = ZS[z]
    for k in range(1, NZ):
        remote(
            ZS.at[0], ZB.at[lax.rem(z + NZ - k, NZ)], zs.at[0], zr.at[k], partner
        ).wait_recv()
    d, gy = y // 4, y % 4
    for j in range(NY):
        yy = lax.rem(y + j, NY)
        YS[j] = ZB[pl.ds(0, NZ), yy, :]
    for k in range(LAYERS):
        for j in range(NY):
            yy = lax.rem(y + j, NY)
            copy = remote(
                YS.at[j],
                MC.at[s, gy, c],
                ys.at[k, j],
                yr.at[s, gy, c],
                (sec(k), (yy * NZ + z) * 2 + d),
            )
            if k or j:
                go(copy)
            else:

                @pl.when(d != c)
                def _():
                    copy.start()

                @pl.when(d == c)
                def _():
                    MC[s, gy, c] = YS[0]

                own_y = copy

    def weight_from(layer, piece):
        ref = (WI.at[layer, wi_half], WO.at[layer, wo_half])[piece]
        return remote(ref, ref, ws.at[0, 0], wr.at[layer, piece], partner)

    def pass_on(layer, piece, k):
        ref = (WI.at[layer, wi_half], WO.at[layer, wo_half])[piece]
        go(remote(ref, ref, vs.at[k, piece], vr.at[layer, piece], partner))

    below, above, across = sec(3), sec(1), sec(2)
    weight_from(below, 0).wait_recv()
    ref = WI.at[below, wi_half]
    go(remote(ref, ref, fs.at[0], wr.at[below, 0], up))
    weight_from(above, 1).wait_recv()
    ref = WO.at[above, wo_half]
    go(remote(ref, ref, fs.at[1], wr.at[above, 1], down))
    pass_on(below, 0, 0)
    pass_on(above, 1, 1)
    weight_from(below, 1).wait_recv()
    pass_on(below, 1, 0)
    weight_from(above, 0).wait_recv()
    pass_on(above, 0, 1)
    for l in range(1, LAYERS):
        got_rows(l)
        build_rows(l)
    for piece in range(2):
        weight_from(across, piece).wait_recv()
        pass_on(across, piece, 2)
    for load in loads[1:]:
        load.wait()

    row_id = lax.broadcasted_iota(jnp.int32, (128, 256), 0)
    lane_id = lax.broadcasted_iota(jnp.int32, (128, 256), 1)
    spread = jnp.where(row_id == lane_id // 16, 1.0, 0.0).astype(BF16)
    spread = jnp.where(row_id < 16, spread, jnp.zeros_like(spread))
    diag = (
        lax.broadcasted_iota(jnp.int32, (HALF, 256), 1) % 16
        == lax.broadcasted_iota(jnp.int32, (HALF, 256), 0) % 16
    )

    def got_cols(layer):
        for g in range(GROUPS):
            for cc in range(2):
                here = jnp.logical_and(s == layer, jnp.logical_and(d == c, gy == g))

                @pl.when(jnp.logical_not(jnp.logical_and(here, c == cc)))
                def _():
                    remote(
                        YS.at[0], MC.at[layer, g, cc], ys.at[0, 0], yr.at[layer, g, cc], partner
                    ).wait_recv()

    def got_weights(layer):
        @pl.when(s != layer)
        def _():
            remote(PB.at[layer], PB.at[layer], pbs.at[0], pbr.at[layer], partner).wait_recv()
            for piece in range(2):
                ref = (WI.at[layer, wi_other], WO.at[layer, wo_other])[piece]
                remote(ref, ref, vs.at[0, 0], vr.at[layer, piece], partner).wait_recv()

    def build_cols(layer):
        for g in range(GROUPS):
            for cc in range(2):
                MN[pl.ds(GROUP * g + cc, 8, stride=2), :] = MC[layer, g, cc]
        taps = MN[...]
        for i in range(ROWS):
            turned = taps if i == 0 else pltpu.roll(taps, 128 - 16 * i, 1)
            wide = jnp.dot(turned.astype(BF16), spread, preferred_element_type=F32)
            wide = jnp.where(diag, wide, 0.0)
            wide = jnp.concatenate([wide, jnp.zeros((HALF, 128), F32)], axis=1)
            if i:
                wide = pltpu.roll(wide, 16 * i, 1)
            wide = wide.astype(BF16)
            for g in range(GROUPS):
                LHS[layer, g, GROUP * i : GROUP * (i + 1), :] = wide[GROUP * g : GROUP * (g + 1)]

    def dense(layer, g):
        field = jnp.dot(
            LHS[layer, g], R[layer, g].reshape(BAND, CH), preferred_element_type=F32
        )
        inverse = lax.rsqrt(jnp.mean(field * field, axis=-1, keepdims=True) + 1e-06)
        normed = (field * inverse * PB[layer, 1:2, 0:CH]).astype(BF16)
        hidden = jax.nn.gelu(
            jnp.dot(normed, WI[layer], preferred_element_type=F32) + PB[layer, 0:1, :],
            approximate=True,
        ).astype(BF16)
        state = (field + jnp.dot(hidden, WO[layer], preferred_element_type=F32)).astype(BF16)
        at = pl.ds(pl.multiple_of(16 + GROUP * g, 16), GROUP)
        for i in range(ROWS):
            S[layer + 1, i, at, :] = state[GROUP * i : GROUP * (i + 1)]

    edge_from = pl.multiple_of(64 - 48 * c, 16)
    edge_to = pl.multiple_of(80 * c, 16)
    edge_in = pl.multiple_of(80 - 80 * c, 16)

    def edge_copy(layer):
        return remote(
            S.at[layer, :, pl.ds(edge_from, 16), :],
            S.at[layer, :, pl.ds(edge_to, 16), :],
            ss.at[layer],
            sr.at[layer],
            partner,
        )

    got_cols(0)
    build_cols(0)
    for layer in range(LAYERS):
        if layer > 0:
            ref = S.at[layer, :, pl.ds(edge_in, 16), :]
            remote(ref, ref, ss.at[layer], sr.at[layer], partner).wait_recv()
            send_row(layer, order(GROUPS - 1))
        got_weights(layer)
        if layer + 1 < LAYERS:
            got_cols(layer + 1)
            build_cols(layer + 1)
        for step in range(GROUPS):
            g = order(step)
            got_halos(layer, g)
            dense(layer, g)
            if layer + 1 < LAYERS:
                if step == GROUPS - 1:
                    go(edge_copy(layer + 1))
                if step > 0:
                    send_row(layer + 1, order(step - 1))

    weights = jnp.broadcast_to(readout[...].astype(F32).reshape(1, CH), (8, CH))
    which = lax.broadcasted_iota(jnp.int32, (8, CH), 0)
    logits = jnp.zeros((8, HALF), F32)
    for i in range(ROWS):
        logits = logits + lax.dot_general(
            jnp.where(which == i, weights, 0.0).astype(BF16),
            S[LAYERS, i, 16 : 16 + HALF, :],
            (((1,), (1,)), ((), ())),
            preferred_element_type=F32,
        )
    values = jax.nn.softplus(jnp.concatenate([logits, logits], axis=1))
    DS[0] = values
    DS[1] = pltpu.roll(values, 4, 0)
    go(remote(DS.at[1 - c], DR, ds, dr, partner))
    remote(DS.at[c], DR, ds, dr, partner).wait_recv()
    cols = lax.broadcasted_iota(jnp.int32, (8, 128), 1)
    out[0] = jnp.where(cols // HALF == c, DS[c], DR[...])[0:4]

    for copy in started:
        copy.wait_send()

    @pl.when(d != c)
    def _():
        own_y.wait_send()

    for layer in range(LAYERS):
        for g in range(GROUPS):

            @pl.when(not_first)
            def _():
                halo(layer, g, 0).wait_send()

            @pl.when(not_last)
            def _():
                halo(layer, g, 1).wait_send()


def on_device(raster, row_coef, col_coef, norm_gain, weight_in, bias_in, weight_out, readout):
    vmem = pl.BlockSpec(memory_space=pltpu.VMEM)
    anywhere = pl.BlockSpec(memory_space=pl.ANY)
    dma = pltpu.SemaphoreType.DMA
    return pl.pallas_call(
        kernel,
        out_shape=jax.ShapeDtypeStruct((1, 4, 128), F32),
        in_specs=[anywhere, vmem, vmem, vmem, anywhere, vmem, anywhere, vmem],
        out_specs=vmem,
        scratch_shapes=[
            pltpu.VMEM((LAYERS + 1, ROWS, 96, CH), BF16),
            pltpu.VMEM((LAYERS, GROUPS, 24, GROUP, CH), BF16),
            pltpu.VMEM((LAYERS, GROUPS, ROWS, GROUP, 128), BF16),
            pltpu.VMEM((LAYERS, GROUPS, 128, BAND), BF16),
            pltpu.VMEM((LAYERS, CH, HID), BF16),
            pltpu.VMEM((LAYERS, HID, CH), BF16),
            pltpu.VMEM((LAYERS, ROWS, 16, 128), F32),
            pltpu.VMEM((128, 128), F32),
            pltpu.VMEM((128, 512), F32),
            pltpu.VMEM((512, 128), F32),
            pltpu.VMEM((NZ, 8, 128), F32),
            pltpu.VMEM((NZ, 8, 128), F32),
            pltpu.VMEM((NY, 8, 128), F32),
            pltpu.VMEM((LAYERS, GROUPS, 2, 8, 128), F32),
            pltpu.VMEM((HALF, 128), F32),
            pltpu.VMEM((LAYERS, 8, HID), F32),
            pltpu.VMEM((2, 8, 128), F32),
            pltpu.VMEM((8, 128), F32),
            dma((3,)),
            dma((NZ,)), dma((NZ,)),
            dma((LAYERS, NY)), dma((LAYERS, GROUPS, 2)),
            dma((7,)), dma((LAYERS, 2)),
            dma, dma,
            dma((LAYERS,)), dma((LAYERS,)),
            dma((2, 2)), dma((LAYERS, 2)), dma((2,)),
            dma((3, 2)), dma((LAYERS, 2)),
            dma((LAYERS, 2, GROUPS)), dma((LAYERS, 2, GROUPS)),
            dma((LAYERS,)), dma((LAYERS,)),
            dma, dma,
        ],
        compiler_params=pltpu.CompilerParams(
            collective_id=0, has_side_effects=True, vmem_limit_bytes=67043328
        ),
        name="forecast",
    )(
        raster, row_coef, jnp.swapaxes(col_coef, 1, 2), norm_gain, weight_in, bias_in, weight_out,
        readout,
    )


def solution(mesh):
    placed = (
        P(None, "space", None, None),
        P("section", None, "space", None),
        P("section", None, "space", None),
        P("section", None),
        P("section", None, None),
        P("section", None),
        P("section", None, None),
        P(),
    )
    return jax.shard_map(
        on_device,
        mesh=mesh,
        in_specs=placed,
        out_specs=P("section", "space", None),
        check_vma=False,
    )
```

```python
import jax
import jax.numpy as jnp
from jax import lax
from jax.experimental import pallas as pl
from jax.experimental.pallas import tpu as pltpu
from jax.sharding import PartitionSpec as P

MESH = pl.DeviceIdType.MESH
F32, BF16 = jnp.float32, jnp.bfloat16
LAYERS, TAPS, RAD = 4, 15, 7
NY, NZ = 8, 8
ROWS = 8
HALF = 64
GROUP = 16
GROUPS = HALF // GROUP
CH, HID = 256, 512
BAND = 24 * GROUP


def remote(src, dst, send_sem, recv_sem, device):
    return pltpu.make_async_remote_copy(
        src_ref=src,
        dst_ref=dst,
        send_sem=send_sem,
        recv_sem=recv_sem,
        device_id=device,
        device_id_type=MESH,
    )


def kernel(
    raster, row_coef, col_coef, gain, w_in, bias, w_out, readout,
    out,
    rcv, ccv, gv, bv, rv, S, R, A, LHS, WI, WO, RC, TT, CS, CT, ZS, ZB, YS, MC, MN, PB, DS, DR,
    lsem, zs, zr, ys, yr, rcs, rcr, ras, rar, pbs, pbr,
    ws, wr, fs, vs, vr, hs, hr, ss, sr, ds, dr,
):
    s = lax.axis_index("section")
    p = lax.axis_index("space")
    t, c = p // 2, p % 2
    y, z = t // NZ, t % NZ
    partner = (s, t * 2 + 1 - c)

    def sec(ds_):
        return lax.rem(s + ds_, LAYERS)

    def dev(yy, zz, cc):
        return (s, (yy * NZ + zz) * 2 + cc)

    prev_chip = (s, lax.rem(t + NY * NZ - 1, NY * NZ) * 2 + c)
    next_chip = (s, lax.rem(t + 1, NY * NZ) * 2 + c)

    d, gy = y // 4, y % 4
    mine = pl.multiple_of(48 * c, 16)
    theirs = pl.multiple_of(48 * (1 - c), 16)
    mine_to = pl.multiple_of(16 - 16 * c, 16)
    theirs_to = pl.multiple_of(16 * c, 16)
    own_rows = pl.ds(c * 4, 4)
    small = [
        pltpu.make_async_copy(src, dst, lsem.at[k])
        for k, (src, dst) in enumerate(
            ((col_coef.at[0, 0], ccv), (row_coef.at[0], rcv), (gain, gv), (bias, bv), (readout, rv))
        )
    ]
    loads = [
        pltpu.make_async_copy(
            raster.at[s, :, pl.ds(mine, 80), :],
            S.at[0, own_rows, pl.ds(mine_to, 80), :],
            lsem.at[5],
        ),
        pltpu.make_async_copy(w_in.at[0], WI.at[s], lsem.at[6]),
        pltpu.make_async_copy(w_out.at[0], WO.at[s], lsem.at[7]),
    ]
    for load in small:
        load.start()

    barrier = pltpu.get_barrier_semaphore()
    greeted = []
    for k in range(LAYERS):
        for j in range(4):
            for cc in range(2):
                greeted.append((sec(k), ((c * 4 + (y + j) % 4) * NZ + z) * 2 + (c + cc) % 2))
    for k in range(1, NZ):
        greeted.append(dev(y, lax.rem(z + k, NZ), c))
    for k in range(1, LAYERS):
        greeted += [(sec(k), t * 2 + c), (sec(k), t * 2 + 1 - c)]
    greeted += [partner, prev_chip, next_chip]
    for k, device in enumerate(greeted):

        def greet():
            pl.semaphore_signal(barrier, inc=1, device_id=device, device_id_type=MESH)

        if k == 0:
            pl.when(d != c)(greet)
        else:
            greet()
    for load in loads:
        load.start()

    CS[TAPS:, :] = jnp.zeros((128 - TAPS, 512), F32)
    small[0].wait()
    CS[0:TAPS, :] = ccv[...].astype(F32)
    for q in range(4):
        CT[128 * q : 128 * (q + 1), :] = CS[:, 128 * q : 128 * (q + 1)].T
    for zz in range(NZ):
        total = CT[pl.ds(8 * zz, 8, stride=64), :]
        for r in range(1, ROWS):
            total = total + pltpu.roll(CT[pl.ds(8 * zz + r, 8, stride=64), :], 16 * r, 1)
        ZS[zz] = total
    small[1].wait()
    rc = rcv[...].astype(F32)
    for i in range(4):
        RC[s, c * 4 + i] = jnp.concatenate(
            [rc[:, i, :], jnp.zeros((1, 128), F32)], axis=0
        ).astype(BF16)

    pl.semaphore_wait(barrier, len(greeted) - 1 + jnp.where(d != c, 1, 0))

    started = []

    def go(copy):
        copy.start()
        started.append(copy)

    for k in range(1, NZ):
        zz = lax.rem(z + k, NZ)
        go(remote(ZS.at[zz], ZB.at[z], zs.at[k], zr.at[k], dev(y, zz, c)))
    half = pl.ds(c * 4, 4)
    rows_sent = [(s, t * 2 + 1 - c)]
    for k in range(1, LAYERS):
        rows_sent += [(sec(k), t * 2 + c), (sec(k), t * 2 + 1 - c)]
    for k, device in enumerate(rows_sent):
        go(remote(RC.at[s, half], RC.at[s, half], rcs.at[k], rcr.at[s, c], device))
    go(
        remote(
            raster.at[s, :, pl.ds(theirs, 80), :],
            S.at[0, own_rows, pl.ds(theirs_to, 80), :],
            ras,
            rar,
            partner,
        )
    )
    wi_half, wo_half = pl.ds(c * 128, 128), pl.ds(c * 256, 256)
    wi_other, wo_other = pl.ds((1 - c) * 128, 128), pl.ds((1 - c) * 256, 256)
    up, down = (sec(1), p), (sec(3), p)
    for k, device in enumerate((up, down)):
        for piece in (k, 1 - k):
            src = (w_in.at[0, wi_half], w_out.at[0, wo_half])[piece]
            dst = (WI.at[s, wi_half], WO.at[s, wo_half])[piece]
            go(remote(src, dst, ws.at[k, piece], wr.at[s, piece], device))

    for load in small[2:4]:
        load.wait()
    PB[s] = jnp.zeros((8, HID), F32)
    PB[s, 0:1, :] = bv[...].astype(F32)
    PB[s, 1:2, 0:CH] = gv[...].astype(F32)
    for k in range(1, LAYERS):
        go(remote(PB.at[s], PB.at[s], pbs.at[k], pbr.at[s], (sec(k), p)))

    edge = pl.multiple_of(80 * c, 16)

    def clear(layer, carry):
        S[layer, :, pl.ds(edge, 16), :] = jnp.zeros((ROWS, 16, CH), BF16)
        R[layer, :, 22:24] = jnp.zeros((GROUPS, 2, GROUP, CH), BF16)

        @pl.when(t == 0)
        def _():
            R[layer, :, 0:RAD] = jnp.zeros((GROUPS, RAD, GROUP, CH), BF16)

        @pl.when(t == NY * NZ - 1)
        def _():
            R[layer, :, 15:22] = jnp.zeros((GROUPS, RAD, GROUP, CH), BF16)

        return carry

    lax.fori_loop(0, LAYERS, clear, 0)

    def got_rows(layer):
        for h in range(2):

            @pl.when(jnp.logical_or(s != layer, c != h))
            def _():
                ref = RC.at[layer, pl.ds(4 * h, 4)]
                remote(ref, ref, rcs.at[0], rcr.at[layer, h], partner).wait_recv()

    lane = lax.broadcasted_iota(jnp.int32, (HALF, 128), 1)

    def build_rows(layer):
        TT[...] = RC[layer].astype(F32).reshape(128, 128).T
        taps = TT[pl.ds(pl.multiple_of(HALF * c, HALF), HALF), :]
        for i in range(ROWS):
            kept = jnp.where(lane // 16 == i, taps, 0.0)
            for g in range(GROUPS):
                A[layer, g, i] = pltpu.roll(
                    kept[GROUP * g : GROUP * (g + 1)],
                    (9 - 16 * i) % 128,
                    1,
                    stride=1,
                    stride_axis=0,
                ).astype(BF16)

    def row_stencil(layer, g):
        window = pl.ds(pl.multiple_of(GROUP * g, GROUP), 3 * GROUP)
        for i in range(ROWS):
            R[layer, g, RAD + i] = jnp.dot(
                A[layer, g, i][:, 0 : 3 * GROUP],
                S[layer, i, window, :],
                preferred_element_type=F32,
            ).astype(BF16)

    def halo(layer, g, way):
        src, dst, device = ((7, 15, prev_chip), (8, 0, next_chip))[way]
        return remote(
            R.at[layer, g, pl.ds(src, RAD)],
            R.at[layer, g, pl.ds(dst, RAD)],
            hs.at[layer, way, g],
            hr.at[layer, way, g],
            device,
        )

    not_first, not_last = t > 0, t < NY * NZ - 1

    def order(step):
        return jnp.where(c == 0, step, GROUPS - 1 - step)

    def send_row(layer, g):
        row_stencil(layer, g)

        @pl.when(not_first)
        def _():
            halo(layer, g, 0).start()

        @pl.when(not_last)
        def _():
            halo(layer, g, 1).start()

    def got_halos(layer, g):
        @pl.when(not_last)
        def _():
            halo(layer, g, 0).wait_recv()

        @pl.when(not_first)
        def _():
            halo(layer, g, 1).wait_recv()

    def weight_from(layer, piece):
        ref = (WI.at[layer, wi_half], WO.at[layer, wo_half])[piece]
        return remote(ref, ref, ws.at[0, 0], wr.at[layer, piece], partner)

    def pass_on(layer, piece, k):
        ref = (WI.at[layer, wi_half], WO.at[layer, wo_half])[piece]
        go(remote(ref, ref, vs.at[k, piece], vr.at[layer, piece], partner))

    below, above, across = sec(3), sec(1), sec(2)
    ZB[z] = ZS[z]
    for k in range(1, NZ):
        remote(
            ZS.at[0], ZB.at[lax.rem(z + NZ - k, NZ)], zs.at[0], zr.at[k], partner
        ).wait_recv()
    for j in range(NY):
        yy = lax.rem(y + j, NY)
        YS[j] = ZB[pl.ds(0, NZ), yy, :]
    for k in range(LAYERS):
        for j in range(NY):
            yy = lax.rem(y + j, NY)
            copy = remote(
                YS.at[j],
                MC.at[s, gy, c],
                ys.at[k, j],
                yr.at[s, gy, c],
                (sec(k), (yy * NZ + z) * 2 + d),
            )
            if k or j:
                go(copy)
            else:

                @pl.when(d != c)
                def _():
                    copy.start()

                @pl.when(d == c)
                def _():
                    MC[s, gy, c] = YS[0]

                own_y = copy

    weight_from(below, 0).wait_recv()
    ref = WI.at[below, wi_half]
    go(remote(ref, ref, fs.at[0], wr.at[below, 0], up))
    weight_from(above, 1).wait_recv()
    ref = WO.at[above, wo_half]
    go(remote(ref, ref, fs.at[1], wr.at[above, 1], down))
    pass_on(below, 0, 0)
    pass_on(above, 1, 1)
    got_rows(0)
    build_rows(0)
    loads[0].wait()
    their_rows = pl.ds((1 - c) * 4, 4)
    remote(
        raster.at[s, :, pl.ds(theirs, 80), :],
        S.at[0, their_rows, pl.ds(mine_to, 80), :],
        ras,
        rar,
        partner,
    ).wait_recv()
    def first_rows(step, carry):
        send_row(0, order(step))
        return carry

    lax.fori_loop(0, GROUPS, first_rows, 0)

    weight_from(below, 1).wait_recv()
    pass_on(below, 1, 0)
    weight_from(above, 0).wait_recv()
    pass_on(above, 0, 1)
    def later_rows(l, carry):
        got_rows(l)
        build_rows(l)
        return carry

    lax.fori_loop(1, LAYERS, later_rows, 0)
    for piece in range(2):
        weight_from(across, piece).wait_recv()
        pass_on(across, piece, 2)
    for load in loads[1:]:
        load.wait()

    row_id = lax.broadcasted_iota(jnp.int32, (128, 256), 0)
    lane_id = lax.broadcasted_iota(jnp.int32, (128, 256), 1)
    spread = jnp.where(row_id == lane_id // 16, 1.0, 0.0).astype(BF16)
    spread = jnp.where(row_id < 16, spread, jnp.zeros_like(spread))
    diag = (
        lax.broadcasted_iota(jnp.int32, (HALF, 256), 1) % 16
        == lax.broadcasted_iota(jnp.int32, (HALF, 256), 0) % 16
    )

    def got_cols(layer):
        for g in range(GROUPS):
            for cc in range(2):
                here = jnp.logical_and(s == layer, jnp.logical_and(d == c, gy == g))

                @pl.when(jnp.logical_not(jnp.logical_and(here, c == cc)))
                def _():
                    remote(
                        YS.at[0], MC.at[layer, g, cc], ys.at[0, 0], yr.at[layer, g, cc], partner
                    ).wait_recv()

    def got_weights(layer):
        @pl.when(s != layer)
        def _():
            remote(PB.at[layer], PB.at[layer], pbs.at[0], pbr.at[layer], partner).wait_recv()
            for piece in range(2):
                ref = (WI.at[layer, wi_other], WO.at[layer, wo_other])[piece]
                remote(ref, ref, vs.at[0, 0], vr.at[layer, piece], partner).wait_recv()

    def build_cols(layer):
        for g in range(GROUPS):
            for cc in range(2):
                MN[pl.ds(GROUP * g + cc, 8, stride=2), :] = MC[layer, g, cc]
        taps = MN[...]
        for i in range(ROWS):
            turned = taps if i == 0 else pltpu.roll(taps, 128 - 16 * i, 1)
            wide = jnp.dot(turned.astype(BF16), spread, preferred_element_type=F32)
            wide = jnp.where(diag, wide, 0.0)
            wide = jnp.concatenate([wide, jnp.zeros((HALF, 128), F32)], axis=1)
            if i:
                wide = pltpu.roll(wide, 16 * i, 1)
            wide = wide.astype(BF16)
            for g in range(GROUPS):
                LHS[layer, g, GROUP * i : GROUP * (i + 1), :] = wide[GROUP * g : GROUP * (g + 1)]

    def dense(layer, g):
        field = jnp.dot(
            LHS[layer, g], R[layer, g].reshape(BAND, CH), preferred_element_type=F32
        )
        inverse = lax.rsqrt(jnp.mean(field * field, axis=-1, keepdims=True) + 1e-06)
        normed = (field * inverse * PB[layer, 1:2, 0:CH]).astype(BF16)
        hidden = jax.nn.gelu(
            jnp.dot(normed, WI[layer], preferred_element_type=F32) + PB[layer, 0:1, :],
            approximate=True,
        ).astype(BF16)
        state = (field + jnp.dot(hidden, WO[layer], preferred_element_type=F32)).astype(BF16)
        at = pl.ds(pl.multiple_of(16 + GROUP * g, 16), GROUP)
        for i in range(ROWS):
            S[layer + 1, i, at, :] = state[GROUP * i : GROUP * (i + 1)]

    edge_from = pl.multiple_of(64 - 48 * c, 16)
    edge_to = pl.multiple_of(80 * c, 16)
    edge_in = pl.multiple_of(80 - 80 * c, 16)

    def edge_copy(layer):
        return remote(
            S.at[layer, :, pl.ds(edge_from, 16), :],
            S.at[layer, :, pl.ds(edge_to, 16), :],
            ss.at[layer],
            sr.at[layer],
            partner,
        )

    got_cols(0)
    build_cols(0)
    def layer_step(layer, carry):
        @pl.when(layer > 0)
        def _():
            ref = S.at[layer, :, pl.ds(edge_in, 16), :]
            remote(ref, ref, ss.at[layer], sr.at[layer], partner).wait_recv()
            send_row(layer, order(GROUPS - 1))

        got_weights(layer)

        @pl.when(layer + 1 < LAYERS)
        def _():
            got_cols(layer + 1)
            build_cols(layer + 1)

        def group_step(step, carry):
            g = order(step)
            got_halos(layer, g)
            dense(layer, g)

            @pl.when(jnp.logical_and(layer + 1 < LAYERS, step == GROUPS - 1))
            def _():
                edge_copy(layer + 1).start()

            @pl.when(jnp.logical_and(layer + 1 < LAYERS, step > 0))
            def _():
                send_row(layer + 1, order(step - 1))

            return carry

        return lax.fori_loop(0, GROUPS, group_step, carry)

    lax.fori_loop(0, LAYERS, layer_step, 0)

    small[4].wait()
    weights = jnp.broadcast_to(rv[...].astype(F32).reshape(1, CH), (8, CH))
    which = lax.broadcasted_iota(jnp.int32, (8, CH), 0)
    logits = jnp.zeros((8, HALF), F32)
    for i in range(ROWS):
        logits = logits + lax.dot_general(
            jnp.where(which == i, weights, 0.0).astype(BF16),
            S[LAYERS, i, 16 : 16 + HALF, :],
            (((1,), (1,)), ((), ())),
            preferred_element_type=F32,
        )
    values = jax.nn.softplus(jnp.concatenate([logits, logits], axis=1))
    DS[0] = values
    DS[1] = pltpu.roll(values, 4, 0)
    go(remote(DS.at[1 - c], DR, ds, dr, partner))
    remote(DS.at[c], DR, ds, dr, partner).wait_recv()
    cols = lax.broadcasted_iota(jnp.int32, (8, 128), 1)
    out[0] = jnp.where(cols // HALF == c, DS[c], DR[...])[0:4]

    for copy in started:
        copy.wait_send()

    @pl.when(d != c)
    def _():
        own_y.wait_send()

    def drain(layer, carry):
        @pl.when(layer > 0)
        def _():
            edge_copy(layer).wait_send()

        for g in range(GROUPS):

            @pl.when(not_first)
            def _():
                halo(layer, g, 0).wait_send()

            @pl.when(not_last)
            def _():
                halo(layer, g, 1).wait_send()

        return carry

    lax.fori_loop(0, LAYERS, drain, 0)


def on_device(raster, row_coef, col_coef, norm_gain, weight_in, bias_in, weight_out, readout):
    vmem = pl.BlockSpec(memory_space=pltpu.VMEM)
    anywhere = pl.BlockSpec(memory_space=pl.ANY)
    dma = pltpu.SemaphoreType.DMA
    return pl.pallas_call(
        kernel,
        out_shape=jax.ShapeDtypeStruct((1, 4, 128), F32),
        in_specs=[anywhere] * 8,
        out_specs=vmem,
        scratch_shapes=[
            pltpu.VMEM((TAPS, 4, 128), BF16),
            pltpu.VMEM((TAPS, 512), BF16),
            pltpu.VMEM((1, CH), BF16),
            pltpu.VMEM((1, HID), BF16),
            pltpu.VMEM((CH,), BF16),
            pltpu.VMEM((LAYERS + 1, ROWS, 96, CH), BF16),
            pltpu.VMEM((LAYERS, GROUPS, 24, GROUP, CH), BF16),
            pltpu.VMEM((LAYERS, GROUPS, ROWS, GROUP, 128), BF16),
            pltpu.VMEM((LAYERS, GROUPS, 128, BAND), BF16),
            pltpu.VMEM((LAYERS, CH, HID), BF16),
            pltpu.VMEM((LAYERS, HID, CH), BF16),
            pltpu.VMEM((LAYERS, ROWS, 16, 128), BF16),
            pltpu.VMEM((128, 128), F32),
            pltpu.VMEM((128, 512), F32),
            pltpu.VMEM((512, 128), F32),
            pltpu.VMEM((NZ, 8, 128), F32),
            pltpu.VMEM((NZ, 8, 128), F32),
            pltpu.VMEM((NY, 8, 128), F32),
            pltpu.VMEM((LAYERS, GROUPS, 2, 8, 128), F32),
            pltpu.VMEM((HALF, 128), F32),
            pltpu.VMEM((LAYERS, 8, HID), F32),
            pltpu.VMEM((2, 8, 128), F32),
            pltpu.VMEM((8, 128), F32),
            dma((8,)),
            dma((NZ,)), dma((NZ,)),
            dma((LAYERS, NY)), dma((LAYERS, GROUPS, 2)),
            dma((7,)), dma((LAYERS, 2)),
            dma, dma,
            dma((LAYERS,)), dma((LAYERS,)),
            dma((2, 2)), dma((LAYERS, 2)), dma((2,)),
            dma((3, 2)), dma((LAYERS, 2)),
            dma((LAYERS, 2, GROUPS)), dma((LAYERS, 2, GROUPS)),
            dma((LAYERS,)), dma((LAYERS,)),
            dma, dma,
        ],
        compiler_params=pltpu.CompilerParams(
            collective_id=0, has_side_effects=True, vmem_limit_bytes=67043328
        ),
        name="forecast",
    )(
        raster, row_coef, jnp.swapaxes(col_coef, 1, 2), norm_gain, weight_in, bias_in, weight_out,
        readout,
    )


def solution(mesh):
    placed = (
        P(None, "space", None, None),
        P("section", None, "space", None),
        P("section", None, "space", None),
        P("section", None),
        P("section", None, None),
        P("section", None),
        P("section", None, None),
        P(),
    )
    return jax.shard_map(
        on_device,
        mesh=mesh,
        in_specs=placed,
        out_specs=P("section", "space", None),
        check_vma=False,
    )
```

```python
import jax
import jax.numpy as jnp
from jax import lax
from jax.experimental import pallas as pl
from jax.experimental.pallas import tpu as pltpu
from jax.sharding import PartitionSpec as P

MESH = pl.DeviceIdType.MESH
F32, BF16 = jnp.float32, jnp.bfloat16
LAYERS, TAPS, RAD = 4, 15, 7
NY, NZ = 8, 8
ROWS = 8
HALF = 64
GROUP = 16
GROUPS = HALF // GROUP
CH, HID = 256, 512
BAND = 24 * GROUP


def remote(src, dst, send_sem, recv_sem, device):
    return pltpu.make_async_remote_copy(
        src_ref=src,
        dst_ref=dst,
        send_sem=send_sem,
        recv_sem=recv_sem,
        device_id=device,
        device_id_type=MESH,
    )


def kernel(
    raster, row_coef, col_coef, gain, w_in, bias, w_out, readout,
    out,
    rcv, ccv, gv, bv, rv, S, R, A, LHS, WI, WO, RC, TT, CS, CT, ZS, ZB, YS, MC, MN, PB, DS, DR,
    lsem, zs, zr, ys, yr, rcs, rcr, ras, rar, pbs, pbr,
    ws, wr, fs, vs, vr, hs, hr, ss, sr, ds, dr,
):
    s = lax.axis_index("section")
    p = lax.axis_index("space")
    t, c = p // 2, p % 2
    y, z = t // NZ, t % NZ
    partner = (s, t * 2 + 1 - c)

    def sec(ds_):
        return lax.rem(s + ds_, LAYERS)

    def dev(yy, zz, cc):
        return (s, (yy * NZ + zz) * 2 + cc)

    prev_chip = (s, lax.rem(t + NY * NZ - 1, NY * NZ) * 2 + c)
    next_chip = (s, lax.rem(t + 1, NY * NZ) * 2 + c)

    d, gy = y // 4, y % 4
    mine = pl.multiple_of(48 * c, 16)
    theirs = pl.multiple_of(48 * (1 - c), 16)
    mine_to = pl.multiple_of(16 - 16 * c, 16)
    theirs_to = pl.multiple_of(16 * c, 16)
    own_rows = pl.ds(c * 4, 4)
    small = [
        pltpu.make_async_copy(src, dst, lsem.at[k])
        for k, (src, dst) in enumerate(
            ((col_coef.at[0, 0], ccv), (row_coef.at[0], rcv), (gain, gv), (bias, bv), (readout, rv))
        )
    ]
    loads = [
        pltpu.make_async_copy(
            raster.at[s, :, pl.ds(mine, 80), :],
            S.at[0, own_rows, pl.ds(mine_to, 80), :],
            lsem.at[5],
        ),
        pltpu.make_async_copy(w_in.at[0], WI.at[s], lsem.at[6]),
        pltpu.make_async_copy(w_out.at[0], WO.at[s], lsem.at[7]),
    ]
    for load in small:
        load.start()

    barrier = pltpu.get_barrier_semaphore()
    greeted = []
    for k in range(LAYERS):
        for j in range(4):
            for cc in range(2):
                greeted.append((sec(k), ((c * 4 + (y + j) % 4) * NZ + z) * 2 + (c + cc) % 2))
    for k in range(1, NZ):
        greeted.append(dev(y, lax.rem(z + k, NZ), c))
    for k in range(1, LAYERS):
        greeted += [(sec(k), t * 2 + c), (sec(k), t * 2 + 1 - c)]
    greeted += [partner, prev_chip, next_chip]
    for k, device in enumerate(greeted):

        def greet():
            pl.semaphore_signal(barrier, inc=1, device_id=device, device_id_type=MESH)

        if k == 0:
            pl.when(d != c)(greet)
        else:
            greet()
    for load in loads:
        load.start()

    CS[TAPS:, :] = jnp.zeros((128 - TAPS, 512), F32)
    small[0].wait()
    CS[0:TAPS, :] = ccv[...].astype(F32)
    for q in range(4):
        CT[128 * q : 128 * (q + 1), :] = CS[:, 128 * q : 128 * (q + 1)].T
    for zz in range(NZ):
        total = CT[pl.ds(8 * zz, 8, stride=64), :]
        for r in range(1, ROWS):
            total = total + pltpu.roll(CT[pl.ds(8 * zz + r, 8, stride=64), :], 16 * r, 1)
        ZS[zz] = total
    small[1].wait()
    rc = rcv[...].astype(F32)
    for i in range(4):
        RC[s, c * 4 + i] = jnp.concatenate(
            [rc[:, i, :], jnp.zeros((1, 128), F32)], axis=0
        ).astype(BF16)

    pl.semaphore_wait(barrier, len(greeted) - 1 + jnp.where(d != c, 1, 0))

    started = []

    def go(copy):
        copy.start()
        started.append(copy)

    for k in range(1, NZ):
        zz = lax.rem(z + k, NZ)
        go(remote(ZS.at[zz], ZB.at[z], zs.at[k], zr.at[k], dev(y, zz, c)))
    half = pl.ds(c * 4, 4)
    rows_sent = [(s, t * 2 + 1 - c)]
    for k in range(1, LAYERS):
        rows_sent += [(sec(k), t * 2 + c), (sec(k), t * 2 + 1 - c)]
    for k, device in enumerate(rows_sent):
        go(remote(RC.at[s, half], RC.at[s, half], rcs.at[k], rcr.at[s, c], device))
    go(
        remote(
            raster.at[s, :, pl.ds(theirs, 80), :],
            S.at[0, own_rows, pl.ds(theirs_to, 80), :],
            ras,
            rar,
            partner,
        )
    )
    wi_half, wo_half = pl.ds(c * 128, 128), pl.ds(c * 256, 256)
    wi_other, wo_other = pl.ds((1 - c) * 128, 128), pl.ds((1 - c) * 256, 256)
    up, down = (sec(1), p), (sec(3), p)
    for k, device in enumerate((up, down)):
        for piece in (k, 1 - k):
            src = (w_in.at[0, wi_half], w_out.at[0, wo_half])[piece]
            dst = (WI.at[s, wi_half], WO.at[s, wo_half])[piece]
            go(remote(src, dst, ws.at[k, piece], wr.at[s, piece], device))

    for load in small[2:4]:
        load.wait()
    PB[s] = jnp.zeros((8, HID), F32)
    PB[s, 0:1, :] = bv[...].astype(F32)
    PB[s, 1:2, 0:CH] = gv[...].astype(F32)
    for k in range(1, LAYERS):
        go(remote(PB.at[s], PB.at[s], pbs.at[k], pbr.at[s], (sec(k), p)))

    edge = pl.multiple_of(80 * c, 16)

    def clear(layer, carry):
        S[layer, :, pl.ds(edge, 16), :] = jnp.zeros((ROWS, 16, CH), BF16)
        R[layer, :, 22:24] = jnp.zeros((GROUPS, 2, GROUP, CH), BF16)

        @pl.when(t == 0)
        def _():
            R[layer, :, 0:RAD] = jnp.zeros((GROUPS, RAD, GROUP, CH), BF16)

        @pl.when(t == NY * NZ - 1)
        def _():
            R[layer, :, 15:22] = jnp.zeros((GROUPS, RAD, GROUP, CH), BF16)

        return carry

    lax.fori_loop(0, LAYERS, clear, 0)

    def got_rows(layer):
        for h in range(2):

            @pl.when(jnp.logical_or(s != layer, c != h))
            def _():
                ref = RC.at[layer, pl.ds(4 * h, 4)]
                remote(ref, ref, rcs.at[0], rcr.at[layer, h], partner).wait_recv()

    lane = lax.broadcasted_iota(jnp.int32, (HALF, 128), 1)

    def build_rows(layer):
        TT[...] = RC[layer].astype(F32).reshape(128, 128).T
        taps = TT[pl.ds(pl.multiple_of(HALF * c, HALF), HALF), :]
        for i in range(ROWS):
            kept = jnp.where(lane // 16 == i, taps, 0.0)
            for g in range(GROUPS):
                A[layer, g, i] = pltpu.roll(
                    kept[GROUP * g : GROUP * (g + 1)],
                    (9 - 16 * i) % 128,
                    1,
                    stride=1,
                    stride_axis=0,
                ).astype(BF16)

    def row_stencil(layer, g):
        window = pl.ds(pl.multiple_of(GROUP * g, GROUP), 3 * GROUP)
        for i in range(ROWS):
            R[layer, g, RAD + i] = jnp.dot(
                A[layer, g, i][:, 0 : 3 * GROUP],
                S[layer, i, window, :],
                preferred_element_type=F32,
            ).astype(BF16)

    def halo(layer, g, way):
        src, dst, device = ((7, 15, prev_chip), (8, 0, next_chip))[way]
        return remote(
            R.at[layer, g, pl.ds(src, RAD)],
            R.at[layer, g, pl.ds(dst, RAD)],
            hs.at[layer, way, g],
            hr.at[layer, way, g],
            device,
        )

    not_first, not_last = t > 0, t < NY * NZ - 1

    def order(step):
        return jnp.where(c == 0, step, GROUPS - 1 - step)

    def send_row(layer, g):
        row_stencil(layer, g)

        @pl.when(not_first)
        def _():
            halo(layer, g, 0).start()

        @pl.when(not_last)
        def _():
            halo(layer, g, 1).start()

    def got_halos(layer, g):
        @pl.when(not_last)
        def _():
            halo(layer, g, 0).wait_recv()

        @pl.when(not_first)
        def _():
            halo(layer, g, 1).wait_recv()

    def weight_from(layer, piece):
        ref = (WI.at[layer, wi_half], WO.at[layer, wo_half])[piece]
        return remote(ref, ref, ws.at[0, 0], wr.at[layer, piece], partner)

    def pass_on(layer, piece, k):
        ref = (WI.at[layer, wi_half], WO.at[layer, wo_half])[piece]
        go(remote(ref, ref, vs.at[k, piece], vr.at[layer, piece], partner))

    below, above, across = sec(3), sec(1), sec(2)
    ZB[z] = ZS[z]
    for k in range(1, NZ):
        remote(
            ZS.at[0], ZB.at[lax.rem(z + NZ - k, NZ)], zs.at[0], zr.at[k], partner
        ).wait_recv()
    for j in range(NY):
        yy = lax.rem(y + j, NY)
        YS[j] = ZB[pl.ds(0, NZ), yy, :]
    for k in (2, 1, 3, 0):
        for j in (4, 3, 5, 2, 6, 1, 7, 0):
            yy = lax.rem(y + j, NY)
            copy = remote(
                YS.at[j],
                MC.at[s, gy, c],
                ys.at[k, j],
                yr.at[s, gy, c],
                (sec(k), (yy * NZ + z) * 2 + d),
            )
            if k or j:
                go(copy)
            else:

                @pl.when(d != c)
                def _():
                    copy.start()

                @pl.when(d == c)
                def _():
                    MC[s, gy, c] = YS[0]

                own_y = copy

    weight_from(below, 0).wait_recv()
    ref = WI.at[below, wi_half]
    go(remote(ref, ref, fs.at[0], wr.at[below, 0], up))
    weight_from(above, 1).wait_recv()
    ref = WO.at[above, wo_half]
    go(remote(ref, ref, fs.at[1], wr.at[above, 1], down))
    pass_on(below, 0, 0)
    pass_on(above, 1, 1)
    got_rows(0)
    build_rows(0)
    loads[0].wait()
    their_rows = pl.ds((1 - c) * 4, 4)
    remote(
        raster.at[s, :, pl.ds(theirs, 80), :],
        S.at[0, their_rows, pl.ds(mine_to, 80), :],
        ras,
        rar,
        partner,
    ).wait_recv()
    def first_rows(step, carry):
        send_row(0, order(step))
        return carry

    lax.fori_loop(0, GROUPS, first_rows, 0)

    weight_from(below, 1).wait_recv()
    pass_on(below, 1, 0)
    weight_from(above, 0).wait_recv()
    pass_on(above, 0, 1)
    def later_rows(l, carry):
        got_rows(l)
        build_rows(l)
        return carry

    lax.fori_loop(1, LAYERS, later_rows, 0)
    for piece in range(2):
        weight_from(across, piece).wait_recv()
        pass_on(across, piece, 2)
    for load in loads[1:]:
        load.wait()

    row_id = lax.broadcasted_iota(jnp.int32, (128, 256), 0)
    lane_id = lax.broadcasted_iota(jnp.int32, (128, 256), 1)
    spread = jnp.where(row_id == lane_id // 16, 1.0, 0.0).astype(BF16)
    spread = jnp.where(row_id < 16, spread, jnp.zeros_like(spread))
    diag = (
        lax.broadcasted_iota(jnp.int32, (HALF, 256), 1) % 16
        == lax.broadcasted_iota(jnp.int32, (HALF, 256), 0) % 16
    )

    def got_cols(layer):
        for g in range(GROUPS):
            for cc in range(2):
                here = jnp.logical_and(s == layer, jnp.logical_and(d == c, gy == g))

                @pl.when(jnp.logical_not(jnp.logical_and(here, c == cc)))
                def _():
                    remote(
                        YS.at[0], MC.at[layer, g, cc], ys.at[0, 0], yr.at[layer, g, cc], partner
                    ).wait_recv()

    def got_weights(layer):
        @pl.when(s != layer)
        def _():
            remote(PB.at[layer], PB.at[layer], pbs.at[0], pbr.at[layer], partner).wait_recv()
            for piece in range(2):
                ref = (WI.at[layer, wi_other], WO.at[layer, wo_other])[piece]
                remote(ref, ref, vs.at[0, 0], vr.at[layer, piece], partner).wait_recv()

    def build_cols(layer):
        for g in range(GROUPS):
            for cc in range(2):
                MN[pl.ds(GROUP * g + cc, 8, stride=2), :] = MC[layer, g, cc]
        taps = MN[...]
        for i in range(ROWS):
            turned = taps if i == 0 else pltpu.roll(taps, 128 - 16 * i, 1)
            wide = jnp.dot(turned.astype(BF16), spread, preferred_element_type=F32)
            wide = jnp.where(diag, wide, 0.0)
            wide = jnp.concatenate([wide, jnp.zeros((HALF, 128), F32)], axis=1)
            if i:
                wide = pltpu.roll(wide, 16 * i, 1)
            wide = wide.astype(BF16)
            for g in range(GROUPS):
                LHS[layer, g, GROUP * i : GROUP * (i + 1), :] = wide[GROUP * g : GROUP * (g + 1)]

    def dense(layer, g):
        field = jnp.dot(
            LHS[layer, g], R[layer, g].reshape(BAND, CH), preferred_element_type=F32
        )
        inverse = lax.rsqrt(jnp.mean(field * field, axis=-1, keepdims=True) + 1e-06)
        normed = (field * inverse * PB[layer, 1:2, 0:CH]).astype(BF16)
        hidden = jax.nn.gelu(
            jnp.dot(normed, WI[layer], preferred_element_type=F32) + PB[layer, 0:1, :],
            approximate=True,
        ).astype(BF16)
        state = (field + jnp.dot(hidden, WO[layer], preferred_element_type=F32)).astype(BF16)
        at = pl.ds(pl.multiple_of(16 + GROUP * g, 16), GROUP)
        for i in range(ROWS):
            S[layer + 1, i, at, :] = state[GROUP * i : GROUP * (i + 1)]

    edge_from = pl.multiple_of(64 - 48 * c, 16)
    edge_to = pl.multiple_of(80 * c, 16)
    edge_in = pl.multiple_of(80 - 80 * c, 16)

    def edge_copy(layer):
        return remote(
            S.at[layer, :, pl.ds(edge_from, 16), :],
            S.at[layer, :, pl.ds(edge_to, 16), :],
            ss.at[layer],
            sr.at[layer],
            partner,
        )

    got_cols(0)
    build_cols(0)
    def layer_step(layer, carry):
        @pl.when(layer > 0)
        def _():
            ref = S.at[layer, :, pl.ds(edge_in, 16), :]
            remote(ref, ref, ss.at[layer], sr.at[layer], partner).wait_recv()
            send_row(layer, order(GROUPS - 1))

        got_weights(layer)

        @pl.when(layer + 1 < LAYERS)
        def _():
            got_cols(layer + 1)
            build_cols(layer + 1)

        def group_step(step, carry):
            g = order(step)
            got_halos(layer, g)
            dense(layer, g)

            @pl.when(jnp.logical_and(layer + 1 < LAYERS, step == GROUPS - 1))
            def _():
                edge_copy(layer + 1).start()

            @pl.when(jnp.logical_and(layer + 1 < LAYERS, step > 0))
            def _():
                send_row(layer + 1, order(step - 1))

            return carry

        return lax.fori_loop(0, GROUPS, group_step, carry)

    lax.fori_loop(0, LAYERS, layer_step, 0)

    small[4].wait()
    weights = jnp.broadcast_to(rv[...].astype(F32).reshape(1, CH), (8, CH))
    which = lax.broadcasted_iota(jnp.int32, (8, CH), 0)
    logits = jnp.zeros((8, HALF), F32)
    for i in range(ROWS):
        logits = logits + lax.dot_general(
            jnp.where(which == i, weights, 0.0).astype(BF16),
            S[LAYERS, i, 16 : 16 + HALF, :],
            (((1,), (1,)), ((), ())),
            preferred_element_type=F32,
        )
    values = jax.nn.softplus(jnp.concatenate([logits, logits], axis=1))
    DS[0] = values
    DS[1] = pltpu.roll(values, 4, 0)
    to_partner = remote(DS.at[1 - c], DR, ds, dr, partner)
    to_partner.start()

    for copy in started:
        copy.wait_send()

    @pl.when(d != c)
    def _():
        own_y.wait_send()

    def drain(layer, carry):
        @pl.when(layer > 0)
        def _():
            edge_copy(layer).wait_send()

        for g in range(GROUPS):

            @pl.when(not_first)
            def _():
                halo(layer, g, 0).wait_send()

            @pl.when(not_last)
            def _():
                halo(layer, g, 1).wait_send()

        return carry

    lax.fori_loop(0, LAYERS, drain, 0)

    remote(DS.at[c], DR, ds, dr, partner).wait_recv()
    cols = lax.broadcasted_iota(jnp.int32, (8, 128), 1)
    out[0] = jnp.where(cols // HALF == c, DS[c], DR[...])[0:4]
    to_partner.wait_send()


def on_device(raster, row_coef, col_coef, norm_gain, weight_in, bias_in, weight_out, readout):
    vmem = pl.BlockSpec(memory_space=pltpu.VMEM)
    anywhere = pl.BlockSpec(memory_space=pl.ANY)
    dma = pltpu.SemaphoreType.DMA
    return pl.pallas_call(
        kernel,
        out_shape=jax.ShapeDtypeStruct((1, 4, 128), F32),
        in_specs=[anywhere] * 8,
        out_specs=vmem,
        scratch_shapes=[
            pltpu.VMEM((TAPS, 4, 128), BF16),
            pltpu.VMEM((TAPS, 512), BF16),
            pltpu.VMEM((1, CH), BF16),
            pltpu.VMEM((1, HID), BF16),
            pltpu.VMEM((CH,), BF16),
            pltpu.VMEM((LAYERS + 1, ROWS, 96, CH), BF16),
            pltpu.VMEM((LAYERS, GROUPS, 24, GROUP, CH), BF16),
            pltpu.VMEM((LAYERS, GROUPS, ROWS, GROUP, 128), BF16),
            pltpu.VMEM((LAYERS, GROUPS, 128, BAND), BF16),
            pltpu.VMEM((LAYERS, CH, HID), BF16),
            pltpu.VMEM((LAYERS, HID, CH), BF16),
            pltpu.VMEM((LAYERS, ROWS, 16, 128), BF16),
            pltpu.VMEM((128, 128), F32),
            pltpu.VMEM((128, 512), F32),
            pltpu.VMEM((512, 128), F32),
            pltpu.VMEM((NZ, 8, 128), F32),
            pltpu.VMEM((NZ, 8, 128), F32),
            pltpu.VMEM((NY, 8, 128), F32),
            pltpu.VMEM((LAYERS, GROUPS, 2, 8, 128), F32),
            pltpu.VMEM((HALF, 128), F32),
            pltpu.VMEM((LAYERS, 8, HID), F32),
            pltpu.VMEM((2, 8, 128), F32),
            pltpu.VMEM((8, 128), F32),
            dma((8,)),
            dma((NZ,)), dma((NZ,)),
            dma((LAYERS, NY)), dma((LAYERS, GROUPS, 2)),
            dma((7,)), dma((LAYERS, 2)),
            dma, dma,
            dma((LAYERS,)), dma((LAYERS,)),
            dma((2, 2)), dma((LAYERS, 2)), dma((2,)),
            dma((3, 2)), dma((LAYERS, 2)),
            dma((LAYERS, 2, GROUPS)), dma((LAYERS, 2, GROUPS)),
            dma((LAYERS,)), dma((LAYERS,)),
            dma, dma,
        ],
        compiler_params=pltpu.CompilerParams(
            collective_id=0, has_side_effects=True, vmem_limit_bytes=67043328
        ),
        name="forecast",
    )(
        raster, row_coef, jnp.swapaxes(col_coef, 1, 2), norm_gain, weight_in, bias_in, weight_out,
        readout,
    )


def solution(mesh):
    placed = (
        P(None, "space", None, None),
        P("section", None, "space", None),
        P("section", None, "space", None),
        P("section", None),
        P("section", None, None),
        P("section", None),
        P("section", None, None),
        P(),
    )
    return jax.shard_map(
        on_device,
        mesh=mesh,
        in_specs=placed,
        out_specs=P("section", "space", None),
        check_vma=False,
    )
```
